32 devices in a mesh: dp: 8 (over z, y), tensor: 4 (over x, core).
Axes of the slice: x: 2, y: 2, z: 4, core: 2. Of those that a mesh axis runs over, the one named last changes fastest.
Arguments:
- patches: bfloat16 [4096, 1280], P(('dp', 'tensor')), may hold values from -12 to 12
- ln_gain: float32 [1280], replicated, may hold values from 0.5 to 1.5
- ln_bias: float32 [1280], replicated, may hold values from -1.8 to 1.8
- fc1_weight: bfloat16 [5120, 2560], P(None, 'tensor'), may hold values from -0.078125 to 0.078125
- fc1_bias: float32 [2560], P('tensor'), may hold values from -3 to 3
- fc2_weight: bfloat16 [2560, 8192], P('tensor'), may hold values from -0.125 to 0.125
- fc2_bias: float32 [8192], replicated, may hold values from -3 to 3
- image_counts: int32 [32, 4], P(('dp', 'tensor')), may hold values from 0 to 32, as said below
- image_positions: int32 [1024], P(('dp', 'tensor')), may hold values from 0 to 4095, as said below
- text_embeds: bfloat16 [4096, 8192], P(('dp', 'tensor')), may hold values from -6 to 6
- keep_mask: int32 [4096, 8192], P(('dp', 'tensor')), may hold values 0 or 1
- norm_gain: float32 [8192], replicated, may hold values from 0.25 to 1.75
- qkv_weight: bfloat16 [8192, 10240], P('dp', 'tensor'), may hold values from -0.0625 to 0.0625
- qkv_bias: float32 [10240], P('tensor'), may hold values from -3 to 3
Outputs:
- stream: bfloat16 [4096, 8192], P(('dp', 'tensor'))
- queries: bfloat16 [4096, 8192], P('dp', 'tensor')
- keys: bfloat16 [4096, 1024], P('dp', 'tensor')
- values: bfloat16 [4096, 1024], P('dp', 'tensor')
The draws below stay inside these ranges and needn't reach their ends.
Inputs may be any that keep to these rules, and one draw needn't show every extreme that they name: `image_counts`: A multiple of 4. In a shard, the images after its first empty one are empty. The counts of one shard sum to at most 128, which one shard reaches in every draw. `image_positions`: all slots name distinct positions. Position p lies on the device of index p // 128 of dp+tensor. The slots of a shard name positions only on devices with the shard's tensor index, exactly 4 on each of them, so every such device receives 4 slots from each shard.
All inputs are finite; a program needn't handle non-finite values. No bound on the sum of `keep_mask` on one device may be relied on, other than what follows from the above.
Results may differ from the reference program's by a relative error of at most 0.0075.
Values may be sent and summed in bfloat16 or wider, within the bound.
A program may use at most 128 MiB of HBM per device.

```python
import jax
import jax.numpy as jnp
from jax import lax

D = 8192
HEADS = 64
KV_HEADS = 8
HEAD_DIM = 128
VIT = 1280
MERGER_HID = 2560
IMG_DEV = 4
S_DEV = 128
M_DEV = 32
MERGE_IN = 5120
QKV = 10240
CAP = 4
TOKENS = 4096
PATCHES = 4096
N_DP = 8
N_TENSOR = 4
DEVICES = 32


def draw_image_counts(key, part):
    per_image = M_DEV // IMG_DEV
    key_live, key_sizes, key_full = jax.random.split(jax.random.fold_in(key, 11), 3)
    live_images = jax.random.randint(key_live, (DEVICES, 1), 1, IMG_DEV + 1)
    sizes = jax.random.randint(key_sizes, (DEVICES, IMG_DEV), 1, per_image + 1)
    full_shard = jax.random.randint(key_full, (), 0, DEVICES)
    image_idx = jnp.arange(IMG_DEV)[None, :]
    merged = jnp.where(image_idx < live_images, sizes, 0)
    merged = jnp.where(jnp.arange(DEVICES)[:, None] == full_shard, per_image, merged)
    return (4 * merged).astype(jnp.int32)


def draw_image_positions(key, part):
    key_source, key_target = jax.random.split(jax.random.fold_in(key, 23), 2)
    source_perm = jax.vmap(lambda one_key: jax.random.permutation(one_key, M_DEV))(jax.random.split(key_source, DEVICES))
    target_perm = jax.vmap(lambda one_key: jax.random.permutation(one_key, S_DEV))(jax.random.split(key_target, DEVICES))[:, :M_DEV]
    shard_ids = jnp.arange(DEVICES)
    shard_dp = shard_ids // N_TENSOR
    shard_tensor = shard_ids % N_TENSOR
    group_ids = jnp.arange(N_DP)
    within = jnp.arange(CAP)
    receiver = group_ids[None, :, None] * N_TENSOR + shard_tensor[:, None, None] + 0 * within[None, None, :]
    column = shard_dp[:, None, None] * CAP + within[None, None, :] + 0 * group_ids[None, :, None]
    target_row = target_perm[receiver, column]
    position = receiver * S_DEV + target_row
    out_slot = source_perm.reshape(DEVICES, N_DP, CAP)
    shard_index = jnp.broadcast_to(shard_ids[:, None, None], out_slot.shape)
    result = jnp.zeros((DEVICES, M_DEV), jnp.int32).at[shard_index, out_slot].set(position.astype(jnp.int32))
    return result.reshape(-1)


def plant(drawn, stream_key, smallest, high):
    dims = drawn.shape
    index_at = [jax.random.randint(jax.random.fold_in(stream_key, axis), (), 0, dims[axis]) for axis in range(len(dims))]
    drawn = drawn.at[tuple(index_at)].set(smallest)
    longest = dims.index(max(dims))
    index_at[longest] = (index_at[longest] + 1) % dims[longest]
    return drawn.at[tuple(index_at)].set(high)


def steps_of(own_key, dims, cuts, low, largest):
    level = 1.0
    for dim, shards_of in cuts:
        draws = jax.random.uniform(jax.random.fold_in(jax.random.fold_in(own_key, 6), dim), (shards_of,), jnp.float32, low / len(cuts), largest / len(cuts))
        level = level * jnp.repeat(jnp.exp(draws), dims[dim] // shards_of).reshape((-1,) + (1,) * (len(dims) - 1 - dim))
    return level


def normal_values(key, shape, scale, bound, cuts=(), held_as=jnp.bfloat16):
    values = scale * jax.random.normal(key, shape, jnp.float32)
    if cuts:
        values = values * steps_of(key, shape, cuts, -0.22, 0.18)
    return jnp.clip(values, -bound, bound).astype(held_as)


def setup_inputs(seed: int = 0) -> dict:
    seeds = jax.random.split(jax.random.key(seed), 15)
    return {
        "patches": normal_values(seeds[0], (PATCHES, VIT), 2.0, 12.0, ((0, 32),)),
        "ln_gain": jnp.clip(1.0 + 0.1 * jax.random.normal(seeds[1], (VIT,), jnp.float32), 0.5, 1.5),
        "ln_bias": normal_values(seeds[2], (VIT,), 0.3, 1.8, (), jnp.float32),
        "fc1_weight": normal_values(seeds[3], (MERGE_IN, MERGER_HID), MERGE_IN ** -0.5, 0.078125, ((1, 4),)),
        "fc1_bias": normal_values(seeds[4], (MERGER_HID,), 0.5, 3.0, ((0, 4),), jnp.float32),
        "fc2_weight": normal_values(seeds[5], (MERGER_HID, D), MERGER_HID ** -0.5, 0.125, ((0, 4),)),
        "fc2_bias": normal_values(seeds[6], (D,), 0.5, 3.0, (), jnp.float32),
        "image_counts": draw_image_counts(jax.random.fold_in(seeds[14], 71), 0),
        "image_positions": draw_image_positions(jax.random.fold_in(seeds[14], 71), 0),
        "text_embeds": normal_values(seeds[9], (TOKENS, D), 1.0, 6.0, ((0, 32),)),
        "keep_mask": plant((jax.random.randint(seeds[10], (TOKENS, D), 0, 10) < 9).astype(jnp.int32), jax.random.fold_in(seeds[10], 1), 0, 1),
        "norm_gain": jnp.clip(1.0 + 0.15 * jax.random.normal(seeds[11], (D,), jnp.float32), 0.25, 1.75),
        "qkv_weight": normal_values(seeds[12], (D, QKV), D ** -0.5, 0.0625, ((0, 8), (1, 4))),
        "qkv_bias": normal_values(seeds[13], (QKV,), 0.5, 3.0, ((0, 4),), jnp.float32),
    }


KEEP_SCALE = 1.0 / 0.9

def layer_norm(inputs, gain, bias):
    widened = inputs.astype(jnp.float32)
    center = lax.optimization_barrier(jnp.mean(widened, axis=-1, keepdims=True))
    spread = lax.optimization_barrier(jnp.mean((widened - center) * (widened - center), axis=-1, keepdims=True))
    return (widened - center) * lax.rsqrt(spread + 1e-06) * gain + bias

def rms_norm(inputs, gain):
    widened = inputs.astype(jnp.float32)
    inverse = lax.rsqrt(lax.optimization_barrier(jnp.mean(widened * widened, axis=-1, keepdims=True)) + 1e-06)
    return (widened * inverse * gain).astype(jnp.bfloat16)

def reference(patches, ln_gain, ln_bias, fc1_weight, fc1_bias, fc2_weight, fc2_bias, image_counts, image_positions, text_embeds, keep_mask, norm_gain, qkv_weight, qkv_bias):
    patch_normed = layer_norm(patches, ln_gain, ln_bias).astype(jnp.bfloat16)
    merged_in = patch_normed.reshape(-1, 4 * VIT)
    merger_hidden = jax.nn.gelu(jnp.dot(merged_in, fc1_weight, preferred_element_type=jnp.float32) + fc1_bias, approximate=False).astype(jnp.bfloat16)
    hid_rows = MERGER_HID // N_TENSOR
    summed = jnp.zeros((merged_in.shape[0], D), jnp.float32)
    for tensor_idx in range(N_TENSOR):
        lower = tensor_idx * hid_rows
        term = jnp.dot(merger_hidden[:, lower:lower + hid_rows], fc2_weight[lower:lower + hid_rows], preferred_element_type=jnp.float32)
        summed = summed + term.astype(jnp.bfloat16).astype(jnp.float32)
    merged_tokens = (summed + fc2_bias).astype(jnp.bfloat16)
    live_slots = lax.optimization_barrier(jnp.sum(image_counts, axis=1)) // 4
    usable = (jnp.arange(M_DEV, dtype=jnp.int32)[None, :] < live_slots[:, None]).reshape(-1)
    target = jnp.where(usable, image_positions, TOKENS).astype(jnp.int32)
    placed = text_embeds.at[target].set(merged_tokens, mode='drop')
    stream = (placed.astype(jnp.float32) * keep_mask.astype(jnp.float32) * KEEP_SCALE).astype(jnp.bfloat16)
    normed = rms_norm(stream, norm_gain)
    projected = jnp.dot(normed, qkv_weight, preferred_element_type=jnp.float32) + qkv_bias
    grouped = projected.reshape(TOKENS, KV_HEADS, -1)
    query_width = HEADS // KV_HEADS * HEAD_DIM
    queries = grouped[:, :, :query_width].reshape(TOKENS, -1).astype(jnp.bfloat16)
    keys = grouped[:, :, query_width:query_width + HEAD_DIM].reshape(TOKENS, -1).astype(jnp.bfloat16)
    values = grouped[:, :, query_width + HEAD_DIM:].reshape(TOKENS, -1).astype(jnp.bfloat16)
    return (stream, queries, keys, values)
```

```python
import functools

import jax
import jax.numpy as jnp
from jax import lax
from jax.experimental import pallas as pl
from jax.experimental.pallas import tpu as pltpu
from jax.sharding import PartitionSpec as P


HEADS = 64
KV_HEADS = 8
HEAD_DIM = 128


KEEP_SCALE = 1.0 / 0.9


def layer_norm(inputs, gain, bias):
    widened = inputs.astype(jnp.float32)
    center = jnp.mean(widened, axis=-1, keepdims=True)
    spread = jnp.mean((widened - center) * (widened - center), axis=-1, keepdims=True)
    return (widened - center) * lax.rsqrt(spread + 1e-06) * gain + bias


def rms_norm(inputs, gain):
    widened = inputs.astype(jnp.float32)
    inverse = lax.rsqrt(jnp.mean(widened * widened, axis=-1, keepdims=True) + 1e-06)
    return (widened * inverse * gain).astype(jnp.bfloat16)


def swap(block, axis, bits):
    return lax.ppermute(block, axis, [(i, i ^ bits) for i in range(lax.axis_size(axis))])


def merger(rows_in, fc1_weight, fc1_bias, fc2_weight, fc2_bias):
    peers = lax.axis_size("tensor")
    rows = rows_in.shape[0]
    gathered = jnp.concatenate([rows_in] + [swap(rows_in, "tensor", k) for k in range(1, peers)])
    product = jnp.dot(gathered, fc1_weight, preferred_element_type=jnp.float32) + fc1_bias
    hidden = jax.nn.gelu(product, approximate=False).astype(jnp.bfloat16)
    terms = jnp.dot(hidden, fc2_weight, preferred_element_type=jnp.float32).astype(jnp.bfloat16)
    summed = terms[:rows].astype(jnp.float32)
    for k in range(1, peers):
        summed = summed + swap(terms[k * rows : (k + 1) * rows], "tensor", k).astype(jnp.float32)
    return (summed + fc2_bias).astype(jnp.bfloat16)


def route_plan(image_counts, image_positions, rows_here, groups, tensor_devs):
    slot_total = image_positions.shape[0]
    per_peer = slot_total // groups
    live_slots = jnp.sum(image_counts) // 4
    usable = jnp.arange(slot_total, dtype=jnp.int32) < live_slots
    owner_dev = image_positions // rows_here
    owner_group = owner_dev // tensor_devs
    owner_row = jnp.where(usable, image_positions % rows_here, -1)
    member = (owner_group[:, None] == jnp.arange(groups, dtype=jnp.int32)[None, :]).astype(
        jnp.int32
    )
    slot_rank = jnp.sum(member * (jnp.cumsum(member, axis=0) - 1), axis=1)
    out_slot = owner_group * per_peer + slot_rank
    chooser = out_slot[None, :] == jnp.arange(slot_total, dtype=jnp.int32)[:, None]
    send_rows = jnp.sum(jnp.where(chooser, owner_row[None, :], 0), axis=1)
    return (chooser.astype(jnp.bfloat16), send_rows.reshape(groups, per_peer))


def arrange(payload, chooser, groups):
    ordered = jnp.dot(chooser, payload, preferred_element_type=jnp.float32).astype(jnp.bfloat16)
    return ordered.reshape(groups, payload.shape[0] // groups, payload.shape[1])


def land(arrived, arrived_rows, text_rows):
    landing = arrived_rows[None, :] == jnp.arange(text_rows.shape[0], dtype=jnp.int32)[:, None]
    covered = jnp.any(landing, axis=1)
    placed = jnp.dot(
        landing.astype(jnp.bfloat16), arrived, preferred_element_type=jnp.float32
    ).astype(jnp.bfloat16)
    return jnp.where(covered[:, None], placed, text_rows)


def half_weights(weight, half):
    deep = weight.shape[0]
    pieces = [(0, weight)]
    if half != 4:
        return pieces + [(k * deep, swap(weight, "dp", k)) for k in range(1, half)]
    beside, above = swap(weight, "dp", 1), swap(weight, "dp", 2)
    middle = deep // 2
    return pieces + [
        (deep, beside),
        (2 * deep, above),
        (3 * deep, swap(beside[:middle], "dp", 2)),
        (3 * deep + middle, swap(above[middle:], "dp", 1)),
    ]


def spread_rows(rows_here):
    held = {0: rows_here}
    bits = lax.axis_size("tensor") // 2
    while bits:
        held.update({k | bits: swap(block, "tensor", bits) for k, block in list(held.items())})
        bits //= 2
    return [held[k] for k in range(len(held))]


def half_product_kernel(blocks, offsets, place, *refs):
    token_refs = refs[:blocks]
    weight_refs = refs[blocks : blocks + len(offsets)]
    out_ref, tokens = refs[-2:]
    rows = token_refs[0].shape[0]

    @pl.when(pl.program_id(0) == 0)
    def _():
        for k in range(blocks):
            at = pl.multiple_of(lax.bitwise_xor(place[0], k) * rows, rows)
            tokens[pl.ds(at, rows), :] = token_refs[k][...]

    total = None
    for offset, weight_ref in zip(offsets, weight_refs):
        deep = weight_ref.shape[0]
        term = jnp.dot(
            tokens[:, offset : offset + deep],
            weight_ref[...],
            preferred_element_type=jnp.float32,
        )
        total = term if total is None else total + term
    out_ref[...] = total.astype(out_ref.dtype)


def half_product(token_blocks, pieces, place, first, width, held_as, name):
    tile = 2 * HEAD_DIM
    rows, deep = token_blocks[0].shape
    total_rows = rows * len(token_blocks)
    start = first // tile
    return pl.pallas_call(
        functools.partial(
            half_product_kernel, len(token_blocks), [offset for offset, _ in pieces]
        ),
        grid_spec=pltpu.PrefetchScalarGridSpec(
            num_scalar_prefetch=1,
            grid=(width // tile,),
            in_specs=[
                pl.BlockSpec((rows, deep), lambda i, place: (0, 0)) for _ in token_blocks
            ]
            + [
                pl.BlockSpec((block.shape[0], tile), lambda i, place: (0, start + i))
                for _, block in pieces
            ],
            out_specs=pl.BlockSpec((total_rows, tile), lambda i, place: (0, i)),
            scratch_shapes=[pltpu.VMEM((total_rows, deep), jnp.bfloat16)],
        ),
        out_shape=jax.ShapeDtypeStruct((total_rows, width), held_as),
        cost_estimate=pl.CostEstimate(
            flops=2 * total_rows * deep * width,
            bytes_accessed=2 * deep * (width + total_rows),
            transcendentals=0,
        ),
        compiler_params=pltpu.CompilerParams(vmem_limit_bytes=48 * 1024 * 1024),
        name=name,
    )(place, *token_blocks, *[block for _, block in pieces])


def finish_kernel(per_group, tiles, here_ref, bias_ref, *refs):
    there_refs = refs[:-3]
    queries, keys, values = refs[-3:]
    step = pl.program_id(0)
    for group, there_ref in enumerate(there_refs):

        @pl.when(step // tiles == group)
        def _():
            result = here_ref[...] + there_ref[...].astype(jnp.float32) + bias_ref[...]
            rounded = result.astype(jnp.bfloat16)

            @pl.when(step % tiles < tiles - 1)
            def _():
                queries[...] = rounded

            @pl.when(step % tiles == tiles - 1)
            def _():
                keys[...] = rounded[:, :HEAD_DIM]
                values[...] = rounded[:, HEAD_DIM:]


def finish(here, there, bias):
    tile = 2 * HEAD_DIM
    rows, width = here.shape
    groups = len(there)
    tiles = width // groups // tile

    def there_map(group):
        return lambda i: (0, jnp.clip(i - group * tiles, 0, tiles - 1))

    return pl.pallas_call(
        functools.partial(finish_kernel, tiles, tiles),
        grid=(width // tile,),
        in_specs=[
            pl.BlockSpec((rows, tile), lambda i: (0, i)),
            pl.BlockSpec((1, tile), lambda i: (0, i)),
        ]
        + [pl.BlockSpec((rows, tile), there_map(group)) for group in range(groups)],
        out_specs=[
            pl.BlockSpec(
                (rows, tile),
                lambda i: (0, i // tiles * (tiles - 1) + jnp.minimum(i % tiles, tiles - 2)),
            ),
            pl.BlockSpec((rows, HEAD_DIM), lambda i: (0, i // tiles)),
            pl.BlockSpec((rows, HEAD_DIM), lambda i: (0, i // tiles)),
        ],
        out_shape=[
            jax.ShapeDtypeStruct((rows, groups * (tiles - 1) * tile), jnp.bfloat16),
            jax.ShapeDtypeStruct((rows, groups * HEAD_DIM), jnp.bfloat16),
            jax.ShapeDtypeStruct((rows, groups * HEAD_DIM), jnp.bfloat16),
        ],
        name="finish",
    )(here, bias[None, :], *there)


def shards(
    patches,
    ln_gain,
    ln_bias,
    fc1_weight,
    fc1_bias,
    fc2_weight,
    fc2_bias,
    image_counts,
    image_positions,
    text_embeds,
    keep_mask,
    norm_gain,
    qkv_weight,
    qkv_bias,
):
    groups = lax.axis_size("dp")
    rows_here = text_embeds.shape[0]
    half = groups // 2
    pieces = half_weights(qkv_weight, half)
    patch_normed = layer_norm(patches, ln_gain, ln_bias).astype(jnp.bfloat16)
    merged_in = patch_normed.reshape(-1, 4 * patches.shape[1])
    chooser, send_rows = route_plan(
        image_counts, image_positions, rows_here, groups, lax.axis_size("tensor")
    )
    merged_tokens = merger(merged_in, fc1_weight, fc1_bias, fc2_weight, fc2_bias)
    outgoing = arrange(merged_tokens, chooser, groups)
    arrived, arrived_rows = (
        lax.all_to_all(outgoing, "dp", split_axis=0, concat_axis=0, tiled=True),
        lax.all_to_all(send_rows, "dp", split_axis=0, concat_axis=0, tiled=True),
    )
    images = arrived.reshape(-1, arrived.shape[-1])
    placed = land(images, arrived_rows.reshape(-1), text_embeds)
    stream = (placed.astype(jnp.float32) * keep_mask.astype(jnp.float32) * KEEP_SCALE).astype(
        jnp.bfloat16
    )
    normed = rms_norm(stream, norm_gain)
    deep = qkv_weight.shape[0]
    here = lax.axis_index("dp")
    within, mine = here % half, here // half
    own_cols, sent_cols = (
        jnp.concatenate(
            [
                lax.dynamic_slice_in_dim(
                    normed,
                    (side * half + lax.bitwise_xor(within, jnp.int32(k))) * deep,
                    deep,
                    axis=1,
                )
                for k in range(half)
            ],
            axis=1,
        )
        for side in (mine, 1 - mine)
    )
    there_rows = spread_rows(swap(sent_cols, "dp", half))
    own_rows = spread_rows(own_cols)
    place = lax.axis_index("tensor")[None]
    group_width = (HEADS // KV_HEADS + 2) * HEAD_DIM
    columns = qkv_weight.shape[1]
    there = [
        swap(
            half_product(
                there_rows, pieces, place, first, group_width, jnp.bfloat16, "partner_half"
            ),
            "dp",
            half,
        )
        for first in range(0, columns, group_width)
    ]
    own_half = half_product(own_rows, pieces, place, 0, columns, jnp.float32, "own_half")
    queries, keys, values = finish(own_half, there, qkv_bias)
    return (stream, queries, keys, values)


def solution(mesh):
    placed = (
        P(("dp", "tensor"), None),
        P(),
        P(),
        P(None, "tensor"),
        P("tensor"),
        P("tensor", None),
        P(),
        P(("dp", "tensor"), None),
        P(("dp", "tensor")),
        P(("dp", "tensor"), None),
        P(("dp", "tensor"), None),
        P(),
        P("dp", "tensor"),
        P("tensor"),
    )
    return jax.shard_map(
        shards,
        mesh=mesh,
        in_specs=placed,
        out_specs=(
            P(("dp", "tensor"), None),
            P("dp", "tensor"),
            P("dp", "tensor"),
            P("dp", "tensor"),
        ),
        check_vma=False,
    )
```

```python
import functools

import jax
import jax.numpy as jnp
from jax import lax
from jax.experimental import pallas as pl
from jax.experimental.pallas import tpu as pltpu
from jax.sharding import PartitionSpec as P


HEADS = 64
KV_HEADS = 8
HEAD_DIM = 128

CHUNKS = 4

KEEP_SCALE = 1.0 / 0.9


def layer_norm(inputs, gain, bias):
    widened = inputs.astype(jnp.float32)
    center = jnp.mean(widened, axis=-1, keepdims=True)
    spread = jnp.mean((widened - center) * (widened - center), axis=-1, keepdims=True)
    return (widened - center) * lax.rsqrt(spread + 1e-06) * gain + bias


def rms_norm(inputs, gain):
    widened = inputs.astype(jnp.float32)
    inverse = lax.rsqrt(jnp.mean(widened * widened, axis=-1, keepdims=True) + 1e-06)
    return (widened * inverse * gain).astype(jnp.bfloat16)


def swap(block, axis, bits):
    return lax.ppermute(block, axis, [(i, i ^ bits) for i in range(lax.axis_size(axis))])


def merger(rows_in, fc1_weight, fc1_bias, fc2_weight, fc2_bias):
    peers = lax.axis_size("tensor")
    rows = rows_in.shape[0]
    gathered = jnp.concatenate([rows_in] + [swap(rows_in, "tensor", k) for k in range(1, peers)])
    product = jnp.dot(gathered, fc1_weight, preferred_element_type=jnp.float32) + fc1_bias
    hidden = jax.nn.gelu(product, approximate=False).astype(jnp.bfloat16)
    terms = jnp.dot(hidden, fc2_weight, preferred_element_type=jnp.float32).astype(jnp.bfloat16)
    summed = terms[:rows].astype(jnp.float32)
    for k in range(1, peers):
        arrived = swap(terms[k * rows : (k + 1) * rows], "tensor", k)
        summed = summed + arrived.astype(jnp.float32)
    return (summed + fc2_bias).astype(jnp.bfloat16)


def after(value, earlier):
    return lax.optimization_barrier((value, earlier))[0]


def route_plan(image_counts, image_positions, rows_here, groups, tensor_devs):
    slot_total = image_positions.shape[0]
    per_peer = slot_total // groups
    live_slots = jnp.sum(image_counts) // 4
    usable = jnp.arange(slot_total, dtype=jnp.int32) < live_slots
    owner_dev = image_positions // rows_here
    owner_group = owner_dev // tensor_devs
    owner_row = jnp.where(usable, image_positions % rows_here, -1)
    member = (owner_group[:, None] == jnp.arange(groups, dtype=jnp.int32)[None, :]).astype(
        jnp.int32
    )
    slot_rank = jnp.sum(member * (jnp.cumsum(member, axis=0) - 1), axis=1)
    out_slot = owner_group * per_peer + slot_rank
    chooser = out_slot[None, :] == jnp.arange(slot_total, dtype=jnp.int32)[:, None]
    landing = owner_row[:, None] == jnp.arange(rows_here, dtype=jnp.int32)[None, :]
    return chooser.astype(jnp.bfloat16), landing.astype(jnp.bfloat16)


def arrange(payload, chooser, groups):
    ordered = jnp.dot(chooser, payload, preferred_element_type=jnp.float32).astype(jnp.bfloat16)
    return ordered.reshape(groups, payload.shape[0] // groups, payload.shape[1])


def scatter_rows(landing, rows):
    return lax.dot_general(
        landing, rows, (((0,), (0,)), ((), ())), preferred_element_type=jnp.float32
    )


def keep_rows(rows, keep):
    return (rows.astype(jnp.float32) * keep * KEEP_SCALE).astype(jnp.bfloat16)


def chunk_bounds(columns):
    tile = 2 * HEAD_DIM
    tiles = columns // tile
    chunks = min(CHUNKS, tiles)
    sizes = [tiles // chunks + (c < tiles % chunks) for c in range(chunks)]
    starts = [sum(sizes[:c]) * tile for c in range(chunks)]
    return [(start, start + size * tile) for start, size in zip(starts, sizes)]


def assemble_kernel(blocks, place, *refs):
    text_refs = refs[:blocks]
    image_refs = refs[blocks : 2 * blocks]
    landing_refs = refs[2 * blocks : 3 * blocks]
    out_ref = refs[-1]
    rows = text_refs[0].shape[0]
    for k in range(blocks):
        landing = landing_refs[k][...]
        moved = scatter_rows(landing, image_refs[k][...]).astype(out_ref.dtype)
        hits = scatter_rows(landing, jnp.ones(landing.shape, landing.dtype))[:, :1]
        at = pl.multiple_of(lax.bitwise_xor(place[0], k) * rows, rows)
        out_ref[pl.ds(at, rows), :] = jnp.where(hits > 0.5, moved, text_refs[k][...])


def assemble(text_blocks, image_blocks, place):
    blocks = len(text_blocks)
    rows, deep = text_blocks[0].shape
    slots, _ = image_blocks[0].shape
    tile = deep // 4
    return pl.pallas_call(
        functools.partial(assemble_kernel, blocks),
        grid_spec=pltpu.PrefetchScalarGridSpec(
            num_scalar_prefetch=1,
            grid=(deep // tile,),
            in_specs=[pl.BlockSpec((rows, tile), lambda i, place: (0, i))] * blocks
            + [pl.BlockSpec((slots, tile), lambda i, place: (0, i))] * blocks
            + [pl.BlockSpec((slots, rows), lambda i, place: (0, deep // rows))] * blocks,
            out_specs=pl.BlockSpec((blocks * rows, tile), lambda i, place: (0, i)),
        ),
        out_shape=jax.ShapeDtypeStruct((blocks * rows, deep), jnp.bfloat16),
        cost_estimate=pl.CostEstimate(
            flops=0, bytes_accessed=4 * blocks * rows * deep, transcendentals=0
        ),
        name="assemble",
    )(place, *text_blocks, *image_blocks, *image_blocks)


def start_weights(chunk, half):
    return [chunk] + [swap(chunk, "dp", k) for k in (range(1, half) if half != 4 else (1, 2))]


def relay_weights(blocks, half, forward_over, ready):
    if half != 4:
        return blocks
    relayed = blocks[1] if forward_over == 2 else blocks[2]
    return blocks + [swap(after(relayed, ready), "dp", forward_over)]


def spread_rows(rows_here):
    held = {0: rows_here}
    bits = lax.axis_size("tensor") // 2
    while bits:
        held.update({k | bits: swap(block, "tensor", bits) for k, block in list(held.items())})
        bits //= 2
    return [held[k] for k in range(len(held))]


def half_product_kernel(tokens, *refs):
    weight_refs, out_ref = refs[:-1], refs[-1]
    total = None
    for k, weight_ref in enumerate(weight_refs):
        deep = weight_ref.shape[0]
        term = jnp.dot(
            tokens[:, k * deep : (k + 1) * deep],
            weight_ref[...],
            preferred_element_type=jnp.float32,
        )
        total = term if total is None else total + term
    out_ref[...] = total.astype(out_ref.dtype)


def half_product(tokens, pieces, held_as):
    tile = 2 * HEAD_DIM
    rows, deep = tokens.shape
    width = pieces[0].shape[1]
    return pl.pallas_call(
        half_product_kernel,
        grid=(width // tile,),
        in_specs=[pl.BlockSpec((rows, deep), lambda i: (0, 0))]
        + [pl.BlockSpec((block.shape[0], tile), lambda i: (0, i)) for block in pieces],
        out_specs=pl.BlockSpec((rows, tile), lambda i: (0, i)),
        out_shape=jax.ShapeDtypeStruct((rows, width), held_as),
        cost_estimate=pl.CostEstimate(
            flops=2 * rows * deep * width,
            bytes_accessed=2 * deep * (width + rows),
            transcendentals=0,
        ),
        compiler_params=pltpu.CompilerParams(vmem_limit_bytes=48 * 1024 * 1024),
    )(tokens, *pieces)


def finish_kernel(bounds, tiles, bias_ref, *refs):
    chunks = len(bounds)
    here_refs, there_refs = refs[:chunks], refs[chunks : 2 * chunks]
    queries, keys, values = refs[2 * chunks :]
    step = pl.program_id(0)
    for (first, last), here_ref, there_ref in zip(bounds, here_refs, there_refs):

        @pl.when((step >= first) & (step < last))
        def _():
            result = here_ref[...] + there_ref[...].astype(jnp.float32) + bias_ref[...]
            rounded = result.astype(jnp.bfloat16)

            @pl.when(step % tiles < tiles - 1)
            def _():
                queries[...] = rounded

            @pl.when(step % tiles == tiles - 1)
            def _():
                keys[...] = rounded[:, :HEAD_DIM]
                values[...] = rounded[:, HEAD_DIM:]


def finish(here, there, bias):
    tile = 2 * HEAD_DIM
    rows = here[0].shape[0]
    width = bias.shape[0]
    tiles = (HEADS // KV_HEADS + 2) * HEAD_DIM // tile
    groups = width // tile // tiles
    bounds = [(a // tile, b // tile) for a, b in chunk_bounds(width)]

    def chunk_map(first, last):
        return lambda i: (0, jnp.clip(i - first, 0, last - first - 1))

    return pl.pallas_call(
        functools.partial(finish_kernel, bounds, tiles),
        grid=(width // tile,),
        in_specs=[pl.BlockSpec((1, tile), lambda i: (0, i))]
        + [pl.BlockSpec((rows, tile), chunk_map(*edges)) for edges in bounds + bounds],
        out_specs=[
            pl.BlockSpec(
                (rows, tile),
                lambda i: (0, i // tiles * (tiles - 1) + jnp.minimum(i % tiles, tiles - 2)),
            ),
            pl.BlockSpec((rows, HEAD_DIM), lambda i: (0, i // tiles)),
            pl.BlockSpec((rows, HEAD_DIM), lambda i: (0, i // tiles)),
        ],
        out_shape=[
            jax.ShapeDtypeStruct((rows, groups * (tiles - 1) * tile), jnp.bfloat16),
            jax.ShapeDtypeStruct((rows, groups * HEAD_DIM), jnp.bfloat16),
            jax.ShapeDtypeStruct((rows, groups * HEAD_DIM), jnp.bfloat16),
        ],
        name="finish",
    )(bias[None, :], *here, *there)


def k_order(rows, half, deep, extra):
    here = lax.axis_index("dp")
    within, mine = here % half, here // half
    return [
        jnp.concatenate(
            [
                lax.dynamic_slice_in_dim(
                    rows,
                    (side * half + lax.bitwise_xor(within, jnp.int32(k))) * deep,
                    deep,
                    axis=1,
                )
                for k in range(half)
            ]
            + extra,
            axis=1,
        )
        for side in (mine, 1 - mine)
    ]


def shards(
    patches,
    ln_gain,
    ln_bias,
    fc1_weight,
    fc1_bias,
    fc2_weight,
    fc2_bias,
    image_counts,
    image_positions,
    text_embeds,
    keep_mask,
    norm_gain,
    qkv_weight,
    qkv_bias,
):
    groups = lax.axis_size("dp")
    rows_here, width = text_embeds.shape
    half = groups // 2
    deep = qkv_weight.shape[0]
    patch_normed = layer_norm(patches, ln_gain, ln_bias).astype(jnp.bfloat16)
    merged_in = patch_normed.reshape(-1, 4 * patches.shape[1])
    chooser, landing = route_plan(
        image_counts, image_positions, rows_here, groups, lax.axis_size("tensor")
    )
    keep = keep_mask.astype(jnp.float32)
    text_stream = keep_rows(text_embeds, keep)
    text_own, text_sent = k_order(rms_norm(text_stream, norm_gain), half, deep, [])
    text_there = swap(text_sent, "dp", half)

    merged_tokens = merger(merged_in, fc1_weight, fc1_bias, fc2_weight, fc2_bias)
    outgoing = arrange(jnp.concatenate([merged_tokens, landing], axis=1), chooser, groups)
    arrived = lax.all_to_all(outgoing, "dp", split_axis=0, concat_axis=0, tiled=True)
    arrived = arrived.reshape(-1, arrived.shape[-1])
    images, landed = arrived[:, :width], arrived[:, width:]
    image_keep = jnp.dot(
        landed, keep_mask.astype(jnp.bfloat16), preferred_element_type=jnp.float32
    )
    image_stream = keep_rows(images, image_keep)
    image_own, image_sent = k_order(rms_norm(image_stream, norm_gain), half, deep, [landed])
    image_there = swap(image_sent, "dp", half)
    image_there = spread_rows(image_there)
    image_own = spread_rows(image_own)
    covered = jnp.sum(landed.astype(jnp.float32), axis=0) > 0.5
    stream = jnp.where(
        covered[:, None], scatter_rows(landed, image_stream).astype(jnp.bfloat16), text_stream
    )

    blocks = []
    for c, (first, last) in enumerate(chunk_bounds(qkv_weight.shape[1])):
        chunk = qkv_weight[:, first:last]
        blocks.append(start_weights(chunk if c < 2 else after(chunk, outgoing), half))

    place = lax.axis_index("tensor")[None]
    tokens_there = assemble(spread_rows(text_there), image_there, place)
    text_own = spread_rows(after(text_own, outgoing))
    ready = [outgoing, image_sent]
    there, here = [], []
    for c in range(len(blocks)):
        over = 2 if c == 1 else 1
        pieces = relay_weights(blocks[c], half, over, ready[c])
        partial = half_product(tokens_there, pieces, jnp.bfloat16)
        ready.append(partial)
        there.append(swap(partial, "dp", half))
        blocks[c] = pieces
        if c == 1:
            tokens_own = assemble([after(text_own[0], partial)] + text_own[1:], image_own, place)
        if c >= 1:
            for own in range(0 if c == 1 else c, c + 1):
                tokens_own = after(tokens_own, partial)
                here.append(half_product(tokens_own, blocks[own], jnp.float32))
            tokens_there = after(tokens_there, here[-1])
    queries, keys, values = finish(here, there, qkv_bias)
    return (stream, queries, keys, values)


def solution(mesh):
    placed = (
        P(("dp", "tensor"), None),
        P(),
        P(),
        P(None, "tensor"),
        P("tensor"),
        P("tensor", None),
        P(),
        P(("dp", "tensor"), None),
        P(("dp", "tensor")),
        P(("dp", "tensor"), None),
        P(("dp", "tensor"), None),
        P(),
        P("dp", "tensor"),
        P("tensor"),
    )
    return jax.shard_map(
        shards,
        mesh=mesh,
        in_specs=placed,
        out_specs=(
            P(("dp", "tensor"), None),
            P("dp", "tensor"),
            P("dp", "tensor"),
            P("dp", "tensor"),
        ),
        check_vma=False,
    )
```
